32 devices in a mesh: frame: 8 (over z, y), group: 4 (over x, core).
Axes of the slice: x: 2, y: 2, z: 4, core: 2. Of those that a mesh axis runs over, the one named last changes fastest.
Arguments:
- frames: bfloat16 [32, 64, 1920], P(('frame', 'group')), may hold values from -6 to 6
- motion: int32 [32, 2, 4, 120], P(('frame', 'group')), may hold values from -64 to 64
- weights: int32 [32, 4, 120], P(('frame', 'group')), may hold values from 1 to 16
- strip_map: int32 [32], replicated, may hold values from 0 to 31, each once
- prior_image: float32 [32, 4, 3840], P(('frame', 'group')), may hold values from -6 to 6
- prior_weight: float32 [32, 4, 3840], P(('frame', 'group')), may hold values from 100 to 2000
Outputs:
- joined_image: float32 [32, 4, 3840], P(('frame', 'group'))
The draws below stay inside these ranges and needn't reach their ends.
Inputs may be any that keep to these rules, and one draw needn't show every extreme that they name: `motion`: motion offsets are whole numbers in high-resolution pixels. `strip_map`: each strip number appears exactly once.
All inputs are finite; a program needn't handle non-finite values.
Results may differ from the reference program's by a relative error of at most 0.0003.
Values sent between devices are 32-bit elements; how exact they have to be, the bound alone decides.
A program may use at most 256 MiB of HBM per device.

```python
import math
import jax
import jax.numpy as jnp
from jax import lax

FRAME_ROWS = 64
FRAME_COLS = 1920
MAX_SHIFT = 64
FRAMES = 32
STRIPS = 32
GRID_COLS = 3840
STRIP_ROWS = 4


def set_ends(values, key, low, largest):
    shape = values.shape
    place = [jax.random.randint(jax.random.fold_in(key, axis), (), 0, shape[axis]) for axis in range(len(shape))]
    values = values.at[tuple(place)].set(low)
    longest = shape.index(max(shape))
    place[longest] = (place[longest] + 1) % shape[longest]
    return values.at[tuple(place)].set(largest)


def raised(values, rng, source, target, shards_of, factor):
    owner, partner = [(jnp.arange(values.shape[position]) // (values.shape[position] // shards_of)).reshape([-1 if axis == position else 1 for axis in range(values.ndim)]) for position in (source, target)]
    chosen = jax.random.permutation(rng, shards_of)[partner]
    strong = (owner == chosen) | (owner == (partner + shards_of // 2) % shards_of)
    return jnp.where(strong, factor * values, values)


def level_of(rng, shape, cuts, least, largest):
    level = 1.0
    for axis_at, blocks in cuts:
        heights = jax.random.uniform(jax.random.fold_in(jax.random.fold_in(rng, 6), axis_at), (blocks,), jnp.float32, least / len(cuts), largest / len(cuts))
        level = level * jnp.repeat(jnp.exp(heights), shape[axis_at] // blocks).reshape((-1,) + (1,) * (len(shape) - 1 - axis_at))
    return level


def normal_values(key, extent, deviation, limit, split=(), kind=jnp.bfloat16):
    array = jax.random.normal(key, extent, jnp.float32) * deviation
    if len(split) > 0:
        array = level_of(key, extent, split, -0.22, 0.18) * array
    return jnp.clip(array, min=-limit, max=limit).astype(kind)


def heavy_noise(stream_key, extent, spread, limit, pieces, heavy, kind=jnp.bfloat16):
    result = spread * jax.random.normal(stream_key, extent, jnp.float32)
    if pieces:
        result = result * level_of(stream_key, extent, pieces, -0.22, 0.18)
    return jnp.clip(raised(result, jax.random.fold_in(stream_key, 3), *heavy), -limit, limit).astype(kind)


def setup_inputs(seed: int = 0) -> dict:
    key_of = jax.random.split(jax.random.key(seed), 7)
    frames = heavy_noise(key_of[0], (FRAMES, FRAME_ROWS, FRAME_COLS), 1.0, 6.0, ((0, 32),), (0, 1, 32, 2.75))
    motion = set_ends(jax.random.randint(key_of[1], (FRAMES, 2, FRAME_ROWS // 16, FRAME_COLS // 16), 0 - MAX_SHIFT, MAX_SHIFT + 1), jax.random.fold_in(key_of[1], 1), 0 - MAX_SHIFT, MAX_SHIFT).astype(jnp.int32)
    weights = set_ends(jax.random.randint(key_of[2], (FRAMES, FRAME_ROWS // 16, FRAME_COLS // 16), 1, 17), jax.random.fold_in(key_of[2], 1), 1, 16).astype(jnp.int32)
    strip_map = jax.random.permutation(key_of[3], STRIPS).astype(jnp.int32)
    prior_image = normal_values(key_of[4], (STRIPS, STRIP_ROWS, GRID_COLS), 1.0, 6.0, ((0, 32),), jnp.float32)
    prior_weight = jnp.clip(jnp.exp(math.log(2000.0) - 2.9957323 * jax.random.uniform(key_of[5], (STRIPS, STRIP_ROWS, GRID_COLS), jnp.float32) ** level_of(key_of[5], (STRIPS, STRIP_ROWS, GRID_COLS), ((0, 32),), -0.2, 0.2)), 100.0, 2000.0)
    return {"frames": frames, "motion": motion, "weights": weights, "strip_map": strip_map, "prior_image": prior_image, "prior_weight": prior_weight}


def upsample(low_frame):
    signal = low_frame.astype(jnp.float32)
    upper_row = jnp.concatenate([signal[:1], signal[:-1]], axis=0)
    lower_row = jnp.concatenate([signal[1:], signal[-1:]], axis=0)
    signal = jnp.stack([0.75 * signal + 0.25 * upper_row, 0.75 * signal + 0.25 * lower_row], axis=1)
    signal = signal.reshape(2 * low_frame.shape[0], low_frame.shape[1])
    left_col = jnp.concatenate([signal[:, :1], signal[:, :-1]], axis=1)
    right_col = jnp.concatenate([signal[:, 1:], signal[:, -1:]], axis=1)
    signal = jnp.stack([0.75 * signal + 0.25 * left_col, 0.75 * signal + 0.25 * right_col], axis=2)
    return signal.reshape(signal.shape[0], 2 * low_frame.shape[1])


def targets(shifts, weight, frame_rows, frame_cols):
    grid_rows = 2 * frame_rows
    grid_cols = 2 * frame_cols
    shift_rows = jnp.repeat(jnp.repeat(shifts[0], 32, axis=0), 32, axis=1).astype(jnp.int32)
    shift_cols = jnp.repeat(jnp.repeat(shifts[1], 32, axis=0), 32, axis=1).astype(jnp.int32)
    weight_map = jnp.repeat(jnp.repeat(weight, 32, axis=0), 32, axis=1).astype(jnp.float32)
    target_rows = jnp.arange(grid_rows, dtype=jnp.int32)[:, None] + shift_rows
    target_cols = jnp.arange(grid_cols, dtype=jnp.int32)[None, :] + shift_cols
    in_grid = (target_rows >= 0) & (target_rows < grid_rows) & (target_cols >= 0) & (target_cols < grid_cols)
    flat_index = jnp.where(in_grid, target_rows * grid_cols + target_cols, grid_rows * grid_cols)
    return flat_index.reshape(-1).astype(jnp.int32), weight_map.reshape(-1)


def reference(frames, motion, weights, strip_map, prior_image, prior_weight):
    frame_rows = frames.shape[1]
    frame_cols = frames.shape[2]
    grid_cells = 4 * frame_rows * frame_cols

    def add_frame(running, frame_item):
        low_frame, shifts, weight = frame_item
        flat_index, weight_map = targets(shifts, weight, frame_rows, frame_cols)
        values = upsample(low_frame).reshape(-1) * weight_map
        weighted = running[0].at[flat_index].add(values, mode="drop")
        counts = running[1].at[flat_index].add(weight_map, mode="drop")
        return (weighted, counts), None

    initial = (jnp.zeros((grid_cells,), jnp.float32), jnp.zeros((grid_cells,), jnp.float32))
    (weighted, counts), _ = lax.scan(add_frame, initial, (frames, motion, weights))
    strips = strip_map.shape[0]
    strip_order = strip_map.astype(jnp.int32)
    weighted = jnp.take(weighted.reshape(strips, -1, 2 * frame_cols), strip_order, axis=0)
    counts = jnp.take(counts.reshape(strips, -1, 2 * frame_cols), strip_order, axis=0)
    return (weighted + prior_weight * prior_image) / (counts + prior_weight)
```

```python
import functools

import jax
import jax.numpy as jnp
from jax import lax
from jax.experimental import pallas as pl
from jax.experimental.pallas import tpu as pltpu
from jax.sharding import PartitionSpec as P

MAX_SHIFT = 64
BLOCK = 32
LANES = 128
MESH = pl.DeviceIdType.MESH


def part_plan(devices, tiles):
    bits = devices.bit_length() - 1
    rest = list(range(1, bits))
    count = 3
    cuts = [tiles * q // count for q in range(count + 1)]
    return [
        (cuts[q], cuts[q + 1], [0] + rest[q:] + rest[:q])
        for q in range(count)
    ]


def splat_kernel(plan, strip_rows, map_ref, motion_ref, weight_ref, frame_ref, *refs):
    outs = refs[: len(plan)]
    rows_ref, up_ref, val_a, val_b, cnt_a, cnt_b = refs[len(plan):]
    low_rows, low_cols = frame_ref.shape[1:]
    grid_rows = 2 * low_rows
    bands = grid_rows // BLOCK
    strips = map_ref.shape[0]
    for acc in (val_a, val_b, cnt_a, cnt_b):
        def clear(t, carry, acc=acc):
            acc[t] = jnp.zeros(acc.shape[1:], jnp.float32)
            return carry
        lax.fori_loop(0, acc.shape[0], clear, 0)

    r = lax.broadcasted_iota(jnp.int32, (grid_rows, low_rows), 0)
    k = lax.broadcasted_iota(jnp.int32, (grid_rows, low_rows), 1)
    own = r // 2
    near = jnp.clip(own - 1 + 2 * (r % 2), 0, low_rows - 1)
    select = jnp.concatenate([(k == own).astype(jnp.float32), (k == near).astype(jnp.float32)], axis=0)
    picked = jnp.dot(select.astype(jnp.bfloat16), frame_ref[0], preferred_element_type=jnp.float32)
    rows_ref[:, LANES : LANES + low_cols] = picked.astype(jnp.bfloat16)
    rows_ref[:, :LANES] = jnp.broadcast_to(picked[:, :1], (2 * grid_rows, LANES)).astype(jnp.bfloat16)
    rows_ref[:, LANES + low_cols :] = jnp.broadcast_to(
        picked[:, low_cols - 1 :], (2 * grid_rows, LANES)
    ).astype(jnp.bfloat16)
    kk = lax.broadcasted_iota(jnp.int32, (3 * LANES, 2 * LANES), 0)
    nn = lax.broadcasted_iota(jnp.int32, (3 * LANES, 2 * LANES), 1)
    mid = nn // 2 + LANES
    spread = jnp.where(kk == mid, 0.75, jnp.where(kk == mid - 1 + 2 * (nn % 2), 0.25, 0.0)).astype(jnp.bfloat16)
    lane = lax.broadcasted_iota(jnp.int32, (BLOCK, LANES), 1)

    def low_tile(u, carry):
        z = jnp.dot(
            rows_ref[:, pl.ds(pl.multiple_of(u * LANES, LANES), 3 * LANES)], spread,
            preferred_element_type=jnp.float32,
        )
        up_ref[...] = 0.75 * z[:grid_rows] + 0.25 * z[grid_rows:]
        for half in range(2):
            for j in range(LANES // BLOCK):
                for b in range(bands):
                    column = u * (2 * LANES // BLOCK) + half * (LANES // BLOCK) + j
                    dy = motion_ref[0, 0, b, column]
                    dx = motion_ref[0, 1, b, column]
                    w = weight_ref[0, b, column].astype(jnp.float32)
                    place = LANES + column * BLOCK + dx
                    tile = place // LANES
                    start = place % LANES
                    top = MAX_SHIFT + b * BLOCK + dy
                    block = up_ref[b * BLOCK : (b + 1) * BLOCK, half * LANES : (half + 1) * LANES]
                    block = pltpu.roll(block, (dx + LANES) % LANES, 1) * w
                    in_a = (lane >= start) & (lane < start + BLOCK)
                    in_b = lane < start + BLOCK - LANES
                    at = pl.ds(top, BLOCK)
                    val_a[tile, at, :] += jnp.where(in_a, block, 0.0)
                    val_b[tile + 1, at, :] += jnp.where(in_b, block, 0.0)
                    cnt_a[tile, at, :] += jnp.where(in_a, w, 0.0)
                    cnt_b[tile + 1, at, :] += jnp.where(in_b, w, 0.0)
        return carry

    lax.fori_loop(0, low_cols // LANES, low_tile, 0)

    def strip(s, carry):
        at = pl.ds(MAX_SHIFT + map_ref[s] * strip_rows, strip_rows)
        for (low, high, order), out in zip(plan, outs):
            position = 0
            for bit in order:
                position = position * 2 + (s // 2**bit) % 2
            for t in range(low, high):
                row = (t - low) * strip_rows
                out[position, row : row + strip_rows, :] = val_a[t + 1, at, :] + val_b[t + 1, at, :]
                row += (high - low) * strip_rows
                out[position, row : row + strip_rows, :] = cnt_a[t + 1, at, :] + cnt_b[t + 1, at, :]
        return carry

    lax.fori_loop(0, strips, strip, 0)


def join_kernel(plan, group_size, image_ref, prior_ref, *refs):
    count = len(plan)
    bits = len(plan[0][2])
    parts = refs[:count]
    out_ref = refs[count]
    landed = refs[count + 1 : count + 1 + count * bits]
    send_sem, recv_sem = refs[-2:]
    strip_rows = out_ref.shape[1]
    me = lax.axis_index("frame") * group_size + lax.axis_index("group")

    def partner(bit):
        other = me + 2**bit - 2 * 2**bit * ((me // 2**bit) % 2)
        return (other // group_size, other % group_size)

    barrier = pltpu.get_barrier_semaphore()
    for bit in range(bits):
        pl.semaphore_signal(barrier, inc=1, device_id=partner(bit), device_id_type=MESH)
    pl.semaphore_wait(barrier, bits)

    def source_of(q, stage):
        return parts[q] if stage == 0 else landed[q * bits + stage - 1]

    def copy_of(q, stage):
        source = source_of(q, stage)
        half = source.shape[0] // 2
        bit = plan[q][2][stage]
        mine = (me // 2**bit) % 2
        return pltpu.make_async_remote_copy(
            src_ref=source.at[pl.ds((1 - mine) * half, half)],
            dst_ref=landed[q * bits + stage],
            send_sem=send_sem.at[q, stage],
            recv_sem=recv_sem.at[q, stage],
            device_id=partner(bit),
            device_id_type=MESH,
        )

    copies = {}
    for q in range(count):
        copies[q, 0] = copy_of(q, 0)
        copies[q, 0].start()
    for stage in range(bits):
        for q in range(count):
            copies[q, stage].wait_recv()
            source = source_of(q, stage)
            half = source.shape[0] // 2
            mine = (me // 2 ** plan[q][2][stage]) % 2
            dest = landed[q * bits + stage]

            for i in range(half):
                dest[i] = dest[i] + source[mine * half + i]
            if stage + 1 < bits:
                copies[q, stage + 1] = copy_of(q, stage + 1)
                copies[q, stage + 1].start()
    for q, (low, high, _) in enumerate(plan):
        total = landed[q * bits + bits - 1]
        for t in range(low, high):
            row = (t - low) * strip_rows
            weighted = total[0, row : row + strip_rows, :]
            row += (high - low) * strip_rows
            counts = total[0, row : row + strip_rows, :]
            cols = slice(t * LANES, (t + 1) * LANES)
            prior = prior_ref[0, :, cols]
            out_ref[0, :, cols] = (weighted + prior * image_ref[0, :, cols]) / (counts + prior)
    for copy in copies.values():
        copy.wait_send()


def body(group_size, frames, motion, weights, strip_map, prior_image, prior_weight):
    low_rows, low_cols = frames.shape[1:]
    strips = strip_map.shape[0]
    strip_rows = prior_image.shape[1]
    tiles = 2 * low_cols // LANES
    plan = part_plan(strips, tiles)
    bits = len(plan[0][2])
    vmem = pl.BlockSpec(memory_space=pltpu.VMEM)
    smem = pl.BlockSpec(memory_space=pltpu.SMEM)
    sizes = [2 * (high - low) * strip_rows for low, high, _ in plan]
    acc = pltpu.VMEM((tiles + 3, 2 * low_rows + 2 * MAX_SHIFT, LANES), jnp.float32)
    parts = pl.pallas_call(
        functools.partial(splat_kernel, plan, strip_rows),
        out_shape=[jax.ShapeDtypeStruct((strips, size, LANES), jnp.float32) for size in sizes],
        in_specs=[smem, smem, smem, vmem],
        out_specs=[vmem] * len(plan),
        scratch_shapes=[
            pltpu.VMEM((4 * low_rows, low_cols + 2 * LANES), jnp.bfloat16),
            pltpu.VMEM((2 * low_rows, 2 * LANES), jnp.float32),
            acc, acc, acc, acc,
        ],
        name="splat",
    )(strip_map, motion, weights, frames)
    landed = [
        pltpu.VMEM((strips >> (stage + 1), size, LANES), jnp.float32)
        for size in sizes for stage in range(bits)
    ]
    return pl.pallas_call(
        functools.partial(join_kernel, plan, group_size),
        out_shape=jax.ShapeDtypeStruct(prior_image.shape, jnp.float32),
        in_specs=[vmem] * (2 + len(plan)),
        out_specs=vmem,
        scratch_shapes=landed + [
            pltpu.SemaphoreType.DMA((len(plan), bits)),
            pltpu.SemaphoreType.DMA((len(plan), bits)),
        ],
        compiler_params=pltpu.CompilerParams(collective_id=0, has_side_effects=True),
        name="join",
    )(prior_image, prior_weight, *parts)


def solution(mesh):
    in_specs = (
        P(("frame", "group"), None, None),
        P(("frame", "group"), None, None, None),
        P(("frame", "group"), None, None),
        P(),
        P(("frame", "group"), None, None),
        P(("frame", "group"), None, None),
    )
    out_specs = P(("frame", "group"), None, None)
    return jax.shard_map(
        functools.partial(body, mesh.shape["group"]), mesh=mesh, in_specs=in_specs, out_specs=out_specs,
        check_vma=False,
    )
```

```python
import functools

import jax
import jax.numpy as jnp
from jax import lax
from jax.experimental import pallas as pl
from jax.experimental.pallas import tpu as pltpu
from jax.sharding import PartitionSpec as P

MAX_SHIFT = 64
SIDE = 2
BLOCK = 32
LANES = 128
MESH = pl.DeviceIdType.MESH


def part_plan(devices, tiles):
    bits = devices.bit_length() - 1
    rest = list(range(1, bits - 1))
    count = 3
    plan = [[], []]
    for q in range(count):
        low, high = tiles * q // count, tiles * (q + 1) // count
        middle = min(high, low + ((high - low + 1) // 2 + 1) // 2 * 2)
        turn = q % len(rest)
        order = [0] + rest[turn:] + rest[:turn] + [bits - 1]
        plan[0].append((low, middle, order))
        plan[1].append((middle, high, order))
    return plan[0] + plan[1]


def splat_kernel(
    plan, strip_rows, map_ref, motion_ref, weight_ref, frame_ref, moves_ref, scores_ref, table_ref, *refs
):
    outs = refs[: len(plan)]
    rows_ref, up_ref, val_a, val_b = refs[len(plan):]
    low_rows, low_cols = frame_ref.shape[1:]
    grid_rows = 2 * low_rows
    bands = grid_rows // BLOCK
    strips = map_ref.shape[0]
    block_count = moves_ref.shape[3]
    table_ref[...] = jnp.zeros(table_ref.shape, jnp.int32)
    table_ref[:bands, :block_count] = moves_ref[0, 1]
    table_ref[bands : 2 * bands, :block_count] = moves_ref[0, 0]
    table_ref[2 * bands : 3 * bands, :block_count] = scores_ref[0]
    table_ref[...] = pltpu.roll(table_ref[...], SIDE, 1)
    for acc in (val_a, val_b):
        def clear(t, carry, acc=acc):
            acc[t] = jnp.zeros(acc.shape[1:], jnp.float32)
            return carry
        lax.fori_loop(0, acc.shape[0], clear, 0)

    r = lax.broadcasted_iota(jnp.int32, (grid_rows, low_rows), 0)
    k = lax.broadcasted_iota(jnp.int32, (grid_rows, low_rows), 1)
    own = r // 2
    near = jnp.clip(own - 1 + 2 * (r % 2), 0, low_rows - 1)
    select = jnp.concatenate([(k == own).astype(jnp.float32), (k == near).astype(jnp.float32)], axis=0)
    picked = jnp.dot(select.astype(jnp.bfloat16), frame_ref[0], preferred_element_type=jnp.float32)
    rows_ref[:, LANES : LANES + low_cols] = picked.astype(jnp.bfloat16)
    rows_ref[:, :LANES] = jnp.broadcast_to(picked[:, :1], (2 * grid_rows, LANES)).astype(jnp.bfloat16)
    rows_ref[:, LANES + low_cols :] = jnp.broadcast_to(
        picked[:, low_cols - 1 :], (2 * grid_rows, LANES)
    ).astype(jnp.bfloat16)
    kk = lax.broadcasted_iota(jnp.int32, (3 * LANES, 2 * LANES), 0)
    nn = lax.broadcasted_iota(jnp.int32, (3 * LANES, 2 * LANES), 1)
    mid = nn // 2 + LANES
    spread = jnp.where(kk == mid, 0.75, jnp.where(kk == mid - 1 + 2 * (nn % 2), 0.25, 0.0)).astype(jnp.bfloat16)
    lane = lax.broadcasted_iota(jnp.int32, (BLOCK, LANES), 1)

    def low_tile(u, carry):
        z = jnp.dot(
            rows_ref[:, pl.ds(pl.multiple_of(u * LANES, LANES), 3 * LANES)], spread,
            preferred_element_type=jnp.float32,
        )
        up_ref[...] = 0.75 * z[:grid_rows] + 0.25 * z[grid_rows:]
        for half in range(2):
            for j in range(LANES // BLOCK):
                for b in range(bands):
                    column = u * (2 * LANES // BLOCK) + half * (LANES // BLOCK) + j
                    dy = motion_ref[0, 0, b, column]
                    dx = motion_ref[0, 1, b, column]
                    w = weight_ref[0, b, column].astype(jnp.float32)
                    place = LANES + column * BLOCK + dx
                    tile = place >> 7
                    start = place & (LANES - 1)
                    top = MAX_SHIFT + b * BLOCK + dy
                    block = up_ref[b * BLOCK : (b + 1) * BLOCK, half * LANES : (half + 1) * LANES]
                    block = pltpu.roll(block, dx & (LANES - 1), 1) * w
                    in_a = (lane >= start) & (lane < start + BLOCK)
                    in_b = lane < start + BLOCK - LANES
                    at = pl.ds(top, BLOCK)
                    val_a[tile, at, :] += jnp.where(in_a, block, 0.0)
                    val_b[tile + 1, at, :] += jnp.where(in_b, block, 0.0)
        return carry

    lax.fori_loop(0, low_cols // LANES, low_tile, 0)

    def strip(s, carry):
        at = pl.ds(MAX_SHIFT + map_ref[s] * strip_rows, strip_rows)
        for (low, high, order), out in zip(plan, outs):
            position = 0
            for bit in order:
                position = position * 2 + ((s >> bit) & 1)
            for t in range(low, high):
                row = (t - low) * strip_rows
                out[position, row : row + strip_rows, :] = val_a[t + 1, at, :] + val_b[t + 1, at, :]
        return carry

    lax.fori_loop(0, strips, strip, 0)


def join_kernel(plan, group_size, map_ref, table_ref, image_ref, prior_ref, *refs):
    count = len(plan)
    bits = len(plan[0][2])
    parts = refs[:count]
    out_ref = refs[count]
    landed = refs[count + 1 : count + 1 + count * bits]
    gathered, staged, move_x, move_y, weight, counts, send_sem, recv_sem, table_send, table_recv = refs[
        count + 1 + count * bits :
    ]
    strip_rows = out_ref.shape[1]
    tiles = out_ref.shape[2] // LANES
    devices = gathered.shape[0]
    blocks = staged.shape[1]
    bands = blocks // devices
    me = lax.axis_index("frame") * group_size + lax.axis_index("group")

    def bit_of(bit):
        return (me // 2**bit) % 2

    def partner(bit):
        other = me + 2**bit - 2 * 2**bit * bit_of(bit)
        return (other // group_size, other % group_size)

    barrier = pltpu.get_barrier_semaphore()
    for bit in range(bits):
        pl.semaphore_signal(barrier, inc=1, device_id=partner(bit), device_id_type=MESH)
    pl.semaphore_wait(barrier, bits)

    def source_of(q, stage):
        return parts[q] if stage == 0 else landed[q * bits + stage - 1]

    def copy_of(q, stage):
        source = source_of(q, stage)
        half = source.shape[0] // 2
        bit = plan[q][2][stage]
        return pltpu.make_async_remote_copy(
            src_ref=source.at[pl.ds((1 - bit_of(bit)) * half, half)],
            dst_ref=landed[q * bits + stage],
            send_sem=send_sem.at[q, stage],
            recv_sem=recv_sem.at[q, stage],
            device_id=partner(bit),
            device_id_type=MESH,
        )

    slot = 0
    for step in range(bits):
        slot = slot + bit_of(bits - 1 - step) * 2**step

    def table_copy(step):
        size = 2**step
        window = pl.ds(slot // size * size, size)
        return pltpu.make_async_remote_copy(
            src_ref=table_ref if step == 0 else gathered.at[window],
            dst_ref=gathered.at[slot] if step == 0 else gathered.at[window],
            send_sem=table_send.at[step],
            recv_sem=table_recv.at[step],
            device_id=partner(bits - 1 - step),
            device_id_type=MESH,
        )

    def turn_tables():
        for f in range(devices):
            for c in range(3):
                staged[c, f * bands : (f + 1) * bands, :] = gathered[f, c * bands : (c + 1) * bands, :]
        for low in range(0, blocks, LANES):
            high = min(blocks, low + LANES)
            for c, dest in enumerate((move_x, move_y, weight)):
                dest[:, low:high] = jnp.transpose(staged[c, low:high, :].astype(jnp.float32)).astype(dest.dtype)

    def count_tiles(first, last):
        position = map_ref[me] * strip_rows + lax.broadcasted_iota(jnp.int32, (8, blocks), 0)
        position = position - BLOCK * (lax.broadcasted_iota(jnp.int32, (8, blocks), 1) % bands)
        column = lax.broadcasted_iota(jnp.int32, (LANES, blocks), 0)
        per_tile = LANES // BLOCK

        def tile(t, carry):
            total = jnp.zeros((8, LANES), jnp.float32)
            for i in range(per_tile + 2 * SIDE):
                at = pl.ds(per_tile * t + i, 1)
                rows_in = ((position - move_y[at, :]) & -BLOCK) == 0
                cols_in = ((column - (move_x[at, :] + BLOCK * (i - SIDE))) & -BLOCK) == 0
                total = total + lax.dot_general(
                    jnp.where(rows_in, weight[at, :], 0.0).astype(jnp.bfloat16),
                    jnp.where(cols_in, 1.0, 0.0).astype(jnp.bfloat16),
                    (((1,), (1,)), ((), ())),
                    preferred_element_type=jnp.float32,
                )
            counts[t] = total
            return carry

        lax.fori_loop(first, last, tile, 0)

    copies = {}
    table_copies = [table_copy(step) for step in range(bits)]
    table_copies[0].start()
    for q in range(count):
        copies[q, 0] = copy_of(q, 0)
        copies[q, 0].start()
    gathered[slot] = table_ref[...]
    count_slots = list(range(bits, 2 * bits - 1))
    for stage in range(bits):
        for chunk in range(2):
            for q in range(chunk * count // 2, (chunk + 1) * count // 2):
                copies[q, stage].wait_recv()
                source = source_of(q, stage)
                half = source.shape[0] // 2
                mine = bit_of(plan[q][2][stage])
                dest = landed[q * bits + stage]
                dest[...] = dest[...] + source[pl.ds(mine * half, half)]
                if stage + 1 < bits:
                    copies[q, stage + 1] = copy_of(q, stage + 1)
                    copies[q, stage + 1].start()
            at = 2 * stage + chunk
            step = at - 1
            if 0 <= step < bits:
                table_copies[step].wait_recv()
                if step + 1 < bits:
                    table_copies[step + 1].start()
                else:
                    turn_tables()
            if at in count_slots:
                n = count_slots.index(at)
                count_tiles(tiles * n // len(count_slots), tiles * (n + 1) // len(count_slots))
    for q, (low, high, _) in enumerate(plan):
        total = landed[q * bits + bits - 1]
        for t in range(low, high):
            row = (t - low) * strip_rows
            weighted = total[0, row : row + strip_rows, :]
            cols = slice(t * LANES, (t + 1) * LANES)
            prior = prior_ref[0, :, cols]
            out_ref[0, :, cols] = (weighted + prior * image_ref[0, :, cols]) / (counts[t, :strip_rows, :] + prior)
    for copy in list(copies.values()) + table_copies:
        copy.wait_send()


def body(group_size, frames, motion, weights, strip_map, prior_image, prior_weight):
    low_rows, low_cols = frames.shape[1:]
    strips = strip_map.shape[0]
    strip_rows = prior_image.shape[1]
    tiles = 2 * low_cols // LANES
    plan = part_plan(strips, tiles)
    bits = len(plan[0][2])
    vmem = pl.BlockSpec(memory_space=pltpu.VMEM)
    smem = pl.BlockSpec(memory_space=pltpu.SMEM)
    sizes = [(high - low) * strip_rows for low, high, _ in plan]
    acc = pltpu.VMEM((tiles + 3, 2 * low_rows + 2 * MAX_SHIFT, LANES), jnp.float32)
    bands = motion.shape[2]
    width = -(-(motion.shape[3] + 2 * SIDE) // LANES) * LANES
    table_rows = -(-3 * bands // 8) * 8
    blocks = strips * bands
    table, *parts = pl.pallas_call(
        functools.partial(splat_kernel, plan, strip_rows),
        out_shape=[jax.ShapeDtypeStruct((table_rows, width), jnp.int32)]
        + [jax.ShapeDtypeStruct((strips, size, LANES), jnp.float32) for size in sizes],
        in_specs=[smem, smem, smem, vmem, vmem, vmem],
        out_specs=[vmem] * (1 + len(plan)),
        scratch_shapes=[
            pltpu.VMEM((4 * low_rows, low_cols + 2 * LANES), jnp.bfloat16),
            pltpu.VMEM((2 * low_rows, 2 * LANES), jnp.float32),
            acc, acc,
        ],
        name="splat",
    )(strip_map, motion, weights, frames, motion, weights)
    landed = [
        pltpu.VMEM((strips >> (stage + 1), size, LANES), jnp.float32)
        for size in sizes for stage in range(bits)
    ]
    return pl.pallas_call(
        functools.partial(join_kernel, plan, group_size),
        out_shape=jax.ShapeDtypeStruct(prior_image.shape, jnp.float32),
        in_specs=[smem] + [vmem] * (3 + len(plan)),
        out_specs=vmem,
        scratch_shapes=landed + [
            pltpu.VMEM((strips, table_rows, width), jnp.int32),
            pltpu.VMEM((3, blocks, width), jnp.int32),
            pltpu.VMEM((width, blocks), jnp.int32),
            pltpu.VMEM((width, blocks), jnp.int32),
            pltpu.VMEM((width, blocks), jnp.float32),
            pltpu.VMEM((tiles, 8, LANES), jnp.float32),
            pltpu.SemaphoreType.DMA((len(plan), bits)),
            pltpu.SemaphoreType.DMA((len(plan), bits)),
            pltpu.SemaphoreType.DMA((bits,)),
            pltpu.SemaphoreType.DMA((bits,)),
        ],
        compiler_params=pltpu.CompilerParams(collective_id=0, has_side_effects=True),
        name="join",
    )(strip_map, table, prior_image, prior_weight, *parts)


def solution(mesh):
    in_specs = (
        P(("frame", "group"), None, None),
        P(("frame", "group"), None, None, None),
        P(("frame", "group"), None, None),
        P(),
        P(("frame", "group"), None, None),
        P(("frame", "group"), None, None),
    )
    out_specs = P(("frame", "group"), None, None)
    return jax.shard_map(
        functools.partial(body, mesh.shape["group"]), mesh=mesh, in_specs=in_specs, out_specs=out_specs,
        check_vma=False,
    )
```

```python
import functools

import jax
import jax.numpy as jnp
from jax import lax
from jax.experimental import pallas as pl
from jax.experimental.pallas import tpu as pltpu
from jax.sharding import PartitionSpec as P

MAX_SHIFT = 64
SIDE = 2
BLOCK = 32
LANES = 128
MESH = pl.DeviceIdType.MESH


def part_plan(devices, tiles):
    bits = devices.bit_length() - 1
    rest = list(range(1, bits - 1))
    count = 3
    plan = [[], []]
    for q in range(count):
        low, high = tiles * q // count, tiles * (q + 1) // count
        middle = min(high, low + ((high - low + 1) // 2 + 1) // 2 * 2)
        turn = q % len(rest)
        order = [0] + rest[turn:] + rest[:turn] + [bits - 1]
        plan[0].append((low, middle, order))
        plan[1].append((middle, high, order))
    return plan[0] + plan[1]


def splat_kernel(plan, strip_rows, map_hbm, motion_hbm, weight_hbm, frame_hbm, table_ref, *refs):
    outs = refs[: len(plan)]
    map_ref, motion_ref, weight_ref, moves_ref, scores_ref, rows_ref, up_ref, val_a, val_b, sems = refs[len(plan):]
    low_rows, low_cols = frame_hbm.shape[1:]
    grid_rows = 2 * low_rows
    bands = grid_rows // BLOCK
    strips = map_ref.shape[0]
    moved = [
        (frame_hbm.at[0], rows_ref.at[:, LANES : LANES + low_cols]),
        (motion_hbm, moves_ref), (weight_hbm, scores_ref),
        (motion_hbm, motion_ref), (weight_hbm, weight_ref), (map_hbm, map_ref),
    ]
    moved = [pltpu.make_async_copy(x, y, sems.at[n]) for n, (x, y) in enumerate(moved)]
    for copy in moved:
        copy.start()
    for acc in (val_a, val_b):
        def clear(t, carry, acc=acc):
            acc[t] = jnp.zeros(acc.shape[1:], jnp.float32)
            return carry
        lax.fori_loop(0, acc.shape[0], clear, 0)
    kk = lax.broadcasted_iota(jnp.int32, (3 * LANES, 2 * LANES), 0)
    nn = lax.broadcasted_iota(jnp.int32, (3 * LANES, 2 * LANES), 1)
    mid = (nn >> 1) + LANES
    spread = jnp.where(kk == mid, 0.75, jnp.where(kk == mid - 1 + 2 * (nn & 1), 0.25, 0.0)).astype(jnp.bfloat16)
    for copy in moved:
        copy.wait()
    block_count = moves_ref.shape[3]
    table_ref[...] = jnp.zeros(table_ref.shape, jnp.int32)
    table_ref[:bands, :block_count] = moves_ref[0, 1]
    table_ref[bands : 2 * bands, :block_count] = moves_ref[0, 0]
    table_ref[2 * bands : 3 * bands, :block_count] = scores_ref[0]
    table_ref[...] = pltpu.roll(table_ref[...], SIDE, 1)
    first = rows_ref[:, LANES : 2 * LANES].astype(jnp.float32)[:, :1]
    last = rows_ref[:, low_cols : LANES + low_cols].astype(jnp.float32)[:, LANES - 1 :]
    rows_ref[:, :LANES] = jnp.broadcast_to(first, (low_rows, LANES)).astype(jnp.bfloat16)
    rows_ref[:, LANES + low_cols :] = jnp.broadcast_to(last, (low_rows, LANES)).astype(jnp.bfloat16)
    line = lax.broadcasted_iota(jnp.int32, (low_rows, 2 * LANES), 0)
    lane = lax.broadcasted_iota(jnp.int32, (BLOCK, LANES), 1)

    def low_tile(u, carry):
        z = jnp.dot(
            rows_ref[:, pl.ds(pl.multiple_of(u * LANES, LANES), 3 * LANES)], spread,
            preferred_element_type=jnp.float32,
        )
        above = jnp.where(line == 0, z, pltpu.roll(z, 1, 0))
        below = jnp.where(line == low_rows - 1, z, pltpu.roll(z, low_rows - 1, 0))
        even = 0.75 * z + 0.25 * above
        odd = 0.75 * z + 0.25 * below
        for half in range(2):
            cols = slice(half * LANES, (half + 1) * LANES)
            up_ref[half, pl.ds(0, low_rows, stride=2), :] = even[:, cols]
            up_ref[half, pl.ds(1, low_rows, stride=2), :] = odd[:, cols]
        for half in range(2):
            for j in range(LANES // BLOCK):
                for b in range(bands):
                    column = u * (2 * LANES // BLOCK) + half * (LANES // BLOCK) + j
                    dy = motion_ref[0, 0, b, column]
                    dx = motion_ref[0, 1, b, column]
                    w = weight_ref[0, b, column].astype(jnp.float32)
                    place = LANES + column * BLOCK + dx
                    tile = place >> 7
                    start = place & (LANES - 1)
                    top = MAX_SHIFT + b * BLOCK + dy
                    block = up_ref[half, b * BLOCK : (b + 1) * BLOCK, :]
                    block = pltpu.roll(block, dx & (LANES - 1), 1) * w
                    in_a = (lane >= start) & (lane < start + BLOCK)
                    in_b = lane < start + BLOCK - LANES
                    at = pl.ds(top, BLOCK)
                    val_a[tile, at, :] += jnp.where(in_a, block, 0.0)
                    val_b[tile + 1, at, :] += jnp.where(in_b, block, 0.0)
        return carry

    lax.fori_loop(0, low_cols // LANES, low_tile, 0)

    def strip(s, carry):
        at = pl.ds(MAX_SHIFT + map_ref[s] * strip_rows, strip_rows)
        for (low, high, order), out in zip(plan, outs):
            position = 0
            for bit in order:
                position = position * 2 + ((s >> bit) & 1)
            for t in range(low, high):
                row = (t - low) * strip_rows
                out[position, row : row + strip_rows, :] = val_a[t + 1, at, :] + val_b[t + 1, at, :]
        return carry

    lax.fori_loop(0, strips, strip, 0)


def join_kernel(plan, group_size, map_hbm, table_ref, image_ref, prior_ref, *refs):
    count = len(plan)
    bits = len(plan[0][2])
    parts = refs[:count]
    out_ref = refs[count]
    landed = refs[count + 1 : count + 1 + count * bits]
    map_ref, map_sem, gathered, staged, move_x, move_y, weight, counts, send_sem, recv_sem, table_send, table_recv = refs[
        count + 1 + count * bits :
    ]
    strip_rows = out_ref.shape[1]
    tiles = out_ref.shape[2] // LANES
    devices = gathered.shape[0]
    blocks = staged.shape[1]
    bands = blocks // devices
    me = lax.axis_index("frame") * group_size + lax.axis_index("group")

    def bit_of(bit):
        return (me // 2**bit) % 2

    groups = [list(range(3, bits)), [1, 2], [0]]
    groups = [[bit for bit in group if bit < bits] for group in groups]
    peers = [[sum(2**bit for n, bit in enumerate(g) if d >> n & 1) for d in range(1, 2 ** len(g))] for g in groups]

    def partner(delta):
        other = me
        for bit in range(bits):
            if delta >> bit & 1:
                other = other + 2**bit - 2 * 2**bit * bit_of(bit)
        return (other // group_size, other % group_size)

    map_copy = pltpu.make_async_copy(map_hbm, map_ref, map_sem)
    map_copy.start()
    barrier = pltpu.get_barrier_semaphore()
    greeted = sorted(set(sum(peers, [])) | {2**bit for bit in range(bits)})
    for delta in greeted:
        pl.semaphore_signal(barrier, inc=1, device_id=partner(delta), device_id_type=MESH)
    pl.semaphore_wait(barrier, len(greeted))

    def source_of(q, stage):
        return parts[q] if stage == 0 else landed[q * bits + stage - 1]

    def copy_of(q, stage):
        source = source_of(q, stage)
        half = source.shape[0] // 2
        bit = plan[q][2][stage]
        return pltpu.make_async_remote_copy(
            src_ref=source.at[pl.ds((1 - bit_of(bit)) * half, half)],
            dst_ref=landed[q * bits + stage],
            send_sem=send_sem.at[q, stage],
            recv_sem=recv_sem.at[q, stage],
            device_id=partner(2**bit),
            device_id_type=MESH,
        )

    slot, scale, sizes = 0, 1, []
    for group in groups:
        sizes.append(scale)
        for bit in group:
            slot = slot + bit_of(bit) * scale
            scale = 2 * scale

    def table_copies_of(step):
        size = sizes[step]
        window = pl.ds(slot // size * size, size)
        return [
            pltpu.make_async_remote_copy(
                src_ref=table_ref if step == 0 else gathered.at[window],
                dst_ref=gathered.at[slot] if step == 0 else gathered.at[window],
                send_sem=table_send.at[delta],
                recv_sem=table_recv.at[delta],
                device_id=partner(delta),
                device_id_type=MESH,
            )
            for delta in peers[step]
        ]

    def turn_tables():
        for f in range(devices):
            for c in range(3):
                staged[c, f * bands : (f + 1) * bands, :] = gathered[f, c * bands : (c + 1) * bands, :]
        for low in range(0, blocks, LANES):
            high = min(blocks, low + LANES)
            for c, dest in enumerate((move_x, move_y, weight)):
                dest[:, low:high] = jnp.transpose(staged[c, low:high, :].astype(jnp.float32)).astype(dest.dtype)

    def count_tiles(first, last):
        position = map_ref[me] * strip_rows + lax.broadcasted_iota(jnp.int32, (8, blocks), 0)
        position = position - BLOCK * (lax.broadcasted_iota(jnp.int32, (8, blocks), 1) % bands)
        column = lax.broadcasted_iota(jnp.int32, (LANES, blocks), 0)
        per_tile = LANES // BLOCK

        def tile(t, carry):
            total = jnp.zeros((8, LANES), jnp.float32)
            for i in range(per_tile + 2 * SIDE):
                at = pl.ds(per_tile * t + i, 1)
                rows_in = ((position - move_y[at, :]) & -BLOCK) == 0
                cols_in = ((column - (move_x[at, :] + BLOCK * (i - SIDE))) & -BLOCK) == 0
                total = total + lax.dot_general(
                    jnp.where(rows_in, weight[at, :], 0.0).astype(jnp.bfloat16),
                    jnp.where(cols_in, 1.0, 0.0).astype(jnp.bfloat16),
                    (((1,), (1,)), ((), ())),
                    preferred_element_type=jnp.float32,
                )
            counts[t] = total
            return carry

        lax.fori_loop(first, last, tile, 0)

    copies = {}
    table_copies = [table_copies_of(step) for step in range(len(groups))]
    for copy in table_copies[0]:
        copy.start()
    for q in range(count):
        copies[q, 0] = copy_of(q, 0)
        copies[q, 0].start()
    gathered[slot] = table_ref[...]

    def next_tables(step):
        for copy in table_copies[step]:
            copy.wait_recv()
        if step + 1 < len(groups):
            for copy in table_copies[step + 1]:
                copy.start()

    next_tables(0)
    count_slots = list(range(2, 2 * bits - 2))
    for stage in range(bits):
        for chunk in range(2):
            for q in range(chunk * count // 2, (chunk + 1) * count // 2):
                copies[q, stage].wait_recv()
                source = source_of(q, stage)
                half = source.shape[0] // 2
                mine = bit_of(plan[q][2][stage])
                dest = landed[q * bits + stage]
                dest[...] = dest[...] + source[pl.ds(mine * half, half)]
                if stage + 1 < bits:
                    copies[q, stage + 1] = copy_of(q, stage + 1)
                    copies[q, stage + 1].start()
            at = 2 * stage + chunk
            if at == 1:
                next_tables(1)
            if at == 2:
                next_tables(2)
                map_copy.wait()
                turn_tables()
            if at in count_slots:
                n = count_slots.index(at)
                count_tiles(tiles * n // len(count_slots), tiles * (n + 1) // len(count_slots))
    for q, (low, high, _) in enumerate(plan):
        total = landed[q * bits + bits - 1]
        for t in range(low, high):
            row = (t - low) * strip_rows
            weighted = total[0, row : row + strip_rows, :]
            cols = slice(t * LANES, (t + 1) * LANES)
            prior = prior_ref[0, :, cols]
            out_ref[0, :, cols] = (weighted + prior * image_ref[0, :, cols]) / (counts[t, :strip_rows, :] + prior)
    for copy in list(copies.values()) + sum(table_copies, []):
        copy.wait_send()


def body(group_size, frames, motion, weights, strip_map, prior_image, prior_weight):
    low_rows, low_cols = frames.shape[1:]
    strips = strip_map.shape[0]
    strip_rows = prior_image.shape[1]
    tiles = 2 * low_cols // LANES
    plan = part_plan(strips, tiles)
    bits = len(plan[0][2])
    vmem = pl.BlockSpec(memory_space=pltpu.VMEM)
    hbm = pl.BlockSpec(memory_space=pltpu.HBM)
    sizes = [(high - low) * strip_rows for low, high, _ in plan]
    acc = pltpu.VMEM((tiles + 3, 2 * low_rows + 2 * MAX_SHIFT, LANES), jnp.float32)
    bands = motion.shape[2]
    width = -(-(motion.shape[3] + 2 * SIDE) // LANES) * LANES
    table_rows = -(-3 * bands // 8) * 8
    blocks = strips * bands
    table, *parts = pl.pallas_call(
        functools.partial(splat_kernel, plan, strip_rows),
        out_shape=[jax.ShapeDtypeStruct((table_rows, width), jnp.int32)]
        + [jax.ShapeDtypeStruct((strips, size, LANES), jnp.float32) for size in sizes],
        in_specs=[hbm] * 4,
        out_specs=[vmem] * (1 + len(plan)),
        scratch_shapes=[
            pltpu.SMEM(strip_map.shape, jnp.int32),
            pltpu.SMEM(motion.shape, jnp.int32),
            pltpu.SMEM(weights.shape, jnp.int32),
            pltpu.VMEM(motion.shape, jnp.int32),
            pltpu.VMEM(weights.shape, jnp.int32),
            pltpu.VMEM((low_rows, low_cols + 2 * LANES), jnp.bfloat16),
            pltpu.VMEM((2, 2 * low_rows, LANES), jnp.float32),
            acc, acc,
            pltpu.SemaphoreType.DMA((6,)),
        ],
        compiler_params=pltpu.CompilerParams(vmem_limit_bytes=20 * 2**20),
        name="splat",
    )(strip_map, motion, weights, frames)
    landed = [
        pltpu.VMEM((strips >> (stage + 1), size, LANES), jnp.float32)
        for size in sizes for stage in range(bits)
    ]
    return pl.pallas_call(
        functools.partial(join_kernel, plan, group_size),
        out_shape=jax.ShapeDtypeStruct(prior_image.shape, jnp.float32),
        in_specs=[hbm] + [vmem] * (3 + len(plan)),
        out_specs=vmem,
        scratch_shapes=landed + [
            pltpu.SMEM(strip_map.shape, jnp.int32),
            pltpu.SemaphoreType.DMA(()),
            pltpu.VMEM((strips, table_rows, width), jnp.int32),
            pltpu.VMEM((3, blocks, width), jnp.int32),
            pltpu.VMEM((width, blocks), jnp.int32),
            pltpu.VMEM((width, blocks), jnp.int32),
            pltpu.VMEM((width, blocks), jnp.float32),
            pltpu.VMEM((tiles, 8, LANES), jnp.float32),
            pltpu.SemaphoreType.DMA((len(plan), bits)),
            pltpu.SemaphoreType.DMA((len(plan), bits)),
            pltpu.SemaphoreType.DMA((strips,)),
            pltpu.SemaphoreType.DMA((strips,)),
        ],
        compiler_params=pltpu.CompilerParams(
            collective_id=0, has_side_effects=True, vmem_limit_bytes=16 * 2**20
        ),
        name="join",
    )(strip_map, table, prior_image, prior_weight, *parts)


def solution(mesh):
    in_specs = (
        P(("frame", "group"), None, None),
        P(("frame", "group"), None, None, None),
        P(("frame", "group"), None, None),
        P(),
        P(("frame", "group"), None, None),
        P(("frame", "group"), None, None),
    )
    out_specs = P(("frame", "group"), None, None)
    return jax.shard_map(
        functools.partial(body, mesh.shape["group"]), mesh=mesh, in_specs=in_specs, out_specs=out_specs,
        check_vma=False,
    )
```

```python
import functools

import jax
import jax.numpy as jnp
from jax import lax
from jax.experimental import pallas as pl
from jax.experimental.pallas import tpu as pltpu
from jax.sharding import PartitionSpec as P

MAX_SHIFT = 64
SIDE = 2
BLOCK = 32
LANES = 128
MESH = pl.DeviceIdType.MESH


def part_plan(devices, tiles):
    bits = devices.bit_length() - 1
    rest = list(range(1, bits - 1))
    count = 3
    plan = [[], []]
    for q in range(count):
        low, high = tiles * q // count, tiles * (q + 1) // count
        middle = min(high, low + ((high - low + 1) // 2 + 1) // 2 * 2)
        turn = q % len(rest)
        order = [0] + rest[turn:] + rest[:turn] + [bits - 1]
        plan[0].append((low, middle, order))
        plan[1].append((middle, high, order))
    return plan[0] + plan[1]


def splat_kernel(plan, strip_rows, map_hbm, motion_hbm, weight_hbm, frame_hbm, table_ref, *refs):
    outs = refs[: len(plan)]
    map_ref, motion_ref, weight_ref, moves_ref, scores_ref, rows_ref, up_ref, val_a, val_b, sems = refs[len(plan):]
    low_rows, low_cols = frame_hbm.shape[1:]
    grid_rows = 2 * low_rows
    bands = grid_rows // BLOCK
    strips = map_ref.shape[0]
    moved = [
        (frame_hbm.at[0], rows_ref.at[:, LANES : LANES + low_cols]),
        (motion_hbm, moves_ref), (weight_hbm, scores_ref),
        (motion_hbm, motion_ref), (weight_hbm, weight_ref), (map_hbm, map_ref),
    ]
    moved = [pltpu.make_async_copy(x, y, sems.at[n]) for n, (x, y) in enumerate(moved)]
    for copy in moved:
        copy.start()
    for acc in (val_a, val_b):
        def clear(t, carry, acc=acc):
            acc[t] = jnp.zeros(acc.shape[1:], jnp.float32)
            return carry
        lax.fori_loop(0, acc.shape[0], clear, 0)
    kk = lax.broadcasted_iota(jnp.int32, (3 * LANES, 2 * LANES), 0)
    nn = lax.broadcasted_iota(jnp.int32, (3 * LANES, 2 * LANES), 1)
    mid = (nn >> 1) + LANES
    spread = jnp.where(kk == mid, 0.75, jnp.where(kk == mid - 1 + 2 * (nn & 1), 0.25, 0.0)).astype(jnp.bfloat16)
    for copy in moved:
        copy.wait()
    block_count = moves_ref.shape[3]
    table_ref[...] = jnp.zeros(table_ref.shape, jnp.int32)
    table_ref[:bands, :block_count] = moves_ref[0, 1]
    table_ref[bands : 2 * bands, :block_count] = moves_ref[0, 0]
    table_ref[2 * bands : 3 * bands, :block_count] = scores_ref[0]
    table_ref[...] = pltpu.roll(table_ref[...], SIDE, 1)
    first = rows_ref[:, LANES : 2 * LANES].astype(jnp.float32)[:, :1]
    last = rows_ref[:, low_cols : LANES + low_cols].astype(jnp.float32)[:, LANES - 1 :]
    rows_ref[:, :LANES] = jnp.broadcast_to(first, (low_rows, LANES)).astype(jnp.bfloat16)
    rows_ref[:, LANES + low_cols :] = jnp.broadcast_to(last, (low_rows, LANES)).astype(jnp.bfloat16)
    line = lax.broadcasted_iota(jnp.int32, (low_rows, 2 * LANES), 0)
    lane = lax.broadcasted_iota(jnp.int32, (BLOCK, LANES), 1)

    def low_tile(u, carry):
        z = jnp.dot(
            rows_ref[:, pl.ds(pl.multiple_of(u * LANES, LANES), 3 * LANES)], spread,
            preferred_element_type=jnp.float32,
        )
        above = jnp.where(line == 0, z, pltpu.roll(z, 1, 0))
        below = jnp.where(line == low_rows - 1, z, pltpu.roll(z, low_rows - 1, 0))
        even = 0.75 * z + 0.25 * above
        odd = 0.75 * z + 0.25 * below
        for half in range(2):
            cols = slice(half * LANES, (half + 1) * LANES)
            up_ref[half, pl.ds(0, low_rows, stride=2), :] = even[:, cols]
            up_ref[half, pl.ds(1, low_rows, stride=2), :] = odd[:, cols]
        for half in range(2):
            for j in range(LANES // BLOCK):
                for b in range(bands):
                    column = u * (2 * LANES // BLOCK) + half * (LANES // BLOCK) + j
                    dy = motion_ref[0, 0, b, column]
                    dx = motion_ref[0, 1, b, column]
                    w = weight_ref[0, b, column].astype(jnp.float32)
                    place = LANES + column * BLOCK + dx
                    tile = place >> 7
                    start = place & (LANES - 1)
                    top = MAX_SHIFT + b * BLOCK + dy
                    block = up_ref[half, b * BLOCK : (b + 1) * BLOCK, :]
                    block = pltpu.roll(block, dx & (LANES - 1), 1) * w
                    in_a = (lane >= start) & (lane < start + BLOCK)
                    in_b = lane < start + BLOCK - LANES
                    at = pl.ds(top, BLOCK)
                    val_a[tile, at, :] += jnp.where(in_a, block, 0.0)
                    val_b[tile + 1, at, :] += jnp.where(in_b, block, 0.0)
        return carry

    lax.fori_loop(0, low_cols // LANES, low_tile, 0)

    def strip(s, carry):
        at = pl.ds(MAX_SHIFT + map_ref[s] * strip_rows, strip_rows)
        for (low, high, order), out in zip(plan, outs):
            position = 0
            for bit in order:
                position = position * 2 + ((s >> bit) & 1)
            for t in range(low, high):
                row = (t - low) * strip_rows
                out[position, row : row + strip_rows, :] = val_a[t + 1, at, :] + val_b[t + 1, at, :]
        return carry

    lax.fori_loop(0, strips, strip, 0)


def join_kernel(plan, group_size, map_hbm, table_ref, image_ref, prior_ref, *refs):
    count = len(plan)
    bits = len(plan[0][2])
    parts = refs[:count]
    out_ref = refs[count]
    landed = refs[count + 1 : count + 1 + count * bits]
    map_ref, map_sem, gathered, staged, move_x, move_y, weight, counts, send_sem, recv_sem, table_send, table_recv = refs[
        count + 1 + count * bits :
    ]
    strip_rows = out_ref.shape[1]
    tiles = out_ref.shape[2] // LANES
    devices = gathered.shape[0]
    blocks = staged.shape[1]
    bands = blocks // devices
    me = lax.axis_index("frame") * group_size + lax.axis_index("group")

    def bit_of(bit):
        return (me // 2**bit) % 2

    groups = [list(range(3, bits)), [1, 2], [0]]
    groups = [[bit for bit in group if bit < bits] for group in groups]
    peers = [[sum(2**bit for n, bit in enumerate(g) if d >> n & 1) for d in range(1, 2 ** len(g))] for g in groups]

    def partner(delta):
        other = me
        for bit in range(bits):
            if delta >> bit & 1:
                other = other + 2**bit - 2 * 2**bit * bit_of(bit)
        return (other // group_size, other % group_size)

    map_copy = pltpu.make_async_copy(map_hbm, map_ref, map_sem)
    map_copy.start()
    barrier = pltpu.get_barrier_semaphore()
    greeted = sorted(set(sum(peers, [])) | {2**bit for bit in range(bits)})
    for delta in greeted:
        pl.semaphore_signal(barrier, inc=1, device_id=partner(delta), device_id_type=MESH)
    pl.semaphore_wait(barrier, len(greeted))

    def source_of(q, stage):
        return parts[q] if stage == 0 else landed[q * bits + stage - 1]

    def copy_of(q, stage):
        source = source_of(q, stage)
        half = source.shape[0] // 2
        bit = plan[q][2][stage]
        return pltpu.make_async_remote_copy(
            src_ref=source.at[pl.ds((1 - bit_of(bit)) * half, half)],
            dst_ref=landed[q * bits + stage],
            send_sem=send_sem.at[q, stage],
            recv_sem=recv_sem.at[q, stage],
            device_id=partner(2**bit),
            device_id_type=MESH,
        )

    slot, scale, sizes = 0, 1, []
    for group in groups:
        sizes.append(scale)
        for bit in group:
            slot = slot + bit_of(bit) * scale
            scale = 2 * scale

    def table_copies_of(step):
        size = sizes[step]
        window = pl.ds(slot // size * size, size)
        return [
            pltpu.make_async_remote_copy(
                src_ref=table_ref if step == 0 else gathered.at[window],
                dst_ref=gathered.at[slot] if step == 0 else gathered.at[window],
                send_sem=table_send.at[delta],
                recv_sem=table_recv.at[delta],
                device_id=partner(delta),
                device_id_type=MESH,
            )
            for delta in peers[step]
        ]

    def turn_tables():
        for f in range(devices):
            for c in range(3):
                staged[c, f * bands : (f + 1) * bands, :] = gathered[f, c * bands : (c + 1) * bands, :]
        for low in range(0, blocks, LANES):
            high = min(blocks, low + LANES)
            for c, dest in enumerate((move_x, move_y, weight)):
                dest[:, low:high] = jnp.transpose(staged[c, low:high, :].astype(jnp.float32)).astype(dest.dtype)

    def count_tiles(first, last):
        position = map_ref[me] * strip_rows + lax.broadcasted_iota(jnp.int32, (8, blocks), 0)
        position = position - BLOCK * (lax.broadcasted_iota(jnp.int32, (8, blocks), 1) % bands)
        column = lax.broadcasted_iota(jnp.int32, (LANES, blocks), 0)
        per_tile = LANES // BLOCK

        def tile(t, carry):
            total = jnp.zeros((8, LANES), jnp.float32)
            for i in range(per_tile + 2 * SIDE):
                at = pl.ds(per_tile * t + i, 1)
                rows_in = ((position - move_y[at, :]) & -BLOCK) == 0
                cols_in = ((column - (move_x[at, :] + BLOCK * (i - SIDE))) & -BLOCK) == 0
                total = total + lax.dot_general(
                    jnp.where(rows_in, weight[at, :], 0.0).astype(jnp.bfloat16),
                    jnp.where(cols_in, 1.0, 0.0).astype(jnp.bfloat16),
                    (((1,), (1,)), ((), ())),
                    preferred_element_type=jnp.float32,
                )
            counts[t] = total
            return carry

        lax.fori_loop(first, last, tile, 0)

    copies = {}
    table_copies = [table_copies_of(step) for step in range(len(groups))]
    for copy in table_copies[0]:
        copy.start()
    for q in range(count):
        copies[q, 0] = copy_of(q, 0)
        copies[q, 0].start()
    gathered[slot] = table_ref[...]

    def next_tables(step):
        for copy in table_copies[step]:
            copy.wait_recv()
        if step + 1 < len(groups):
            for copy in table_copies[step + 1]:
                copy.start()

    count_slots = list(range(3, 2 * bits - 1))
    for stage in range(bits):
        for chunk in range(2):
            for q in range(chunk * count // 2, (chunk + 1) * count // 2):
                copies[q, stage].wait_recv()
                source = source_of(q, stage)
                half = source.shape[0] // 2
                mine = bit_of(plan[q][2][stage])
                dest = landed[q * bits + stage]
                dest[...] = dest[...] + source[pl.ds(mine * half, half)]
                if stage + 1 < bits:
                    copies[q, stage + 1] = copy_of(q, stage + 1)
                    copies[q, stage + 1].start()
            at = 2 * stage + chunk
            if at == 1:
                next_tables(0)
            if at == 2:
                next_tables(1)
            if at == 3:
                next_tables(2)
                map_copy.wait()
                turn_tables()
            if at in count_slots:
                n = count_slots.index(at)
                count_tiles(tiles * n // len(count_slots), tiles * (n + 1) // len(count_slots))
    for q, (low, high, _) in enumerate(plan):
        total = landed[q * bits + bits - 1]
        for t in range(low, high):
            row = (t - low) * strip_rows
            weighted = total[0, row : row + strip_rows, :]
            cols = slice(t * LANES, (t + 1) * LANES)
            prior = prior_ref[0, :, cols]
            out_ref[0, :, cols] = (weighted + prior * image_ref[0, :, cols]) / (counts[t, :strip_rows, :] + prior)
    for copy in list(copies.values()) + sum(table_copies, []):
        copy.wait_send()


def body(group_size, frames, motion, weights, strip_map, prior_image, prior_weight):
    low_rows, low_cols = frames.shape[1:]
    strips = strip_map.shape[0]
    strip_rows = prior_image.shape[1]
    tiles = 2 * low_cols // LANES
    plan = part_plan(strips, tiles)
    bits = len(plan[0][2])
    vmem = pl.BlockSpec(memory_space=pltpu.VMEM)
    hbm = pl.BlockSpec(memory_space=pltpu.HBM)
    sizes = [(high - low) * strip_rows for low, high, _ in plan]
    acc = pltpu.VMEM((tiles + 3, 2 * low_rows + 2 * MAX_SHIFT, LANES), jnp.float32)
    bands = motion.shape[2]
    width = -(-(motion.shape[3] + 2 * SIDE) // LANES) * LANES
    table_rows = -(-3 * bands // 8) * 8
    blocks = strips * bands
    table, *parts = pl.pallas_call(
        functools.partial(splat_kernel, plan, strip_rows),
        out_shape=[jax.ShapeDtypeStruct((table_rows, width), jnp.int32)]
        + [jax.ShapeDtypeStruct((strips, size, LANES), jnp.float32) for size in sizes],
        in_specs=[hbm] * 4,
        out_specs=[vmem] * (1 + len(plan)),
        scratch_shapes=[
            pltpu.SMEM(strip_map.shape, jnp.int32),
            pltpu.SMEM(motion.shape, jnp.int32),
            pltpu.SMEM(weights.shape, jnp.int32),
            pltpu.VMEM(motion.shape, jnp.int32),
            pltpu.VMEM(weights.shape, jnp.int32),
            pltpu.VMEM((low_rows, low_cols + 2 * LANES), jnp.bfloat16),
            pltpu.VMEM((2, 2 * low_rows, LANES), jnp.float32),
            acc, acc,
            pltpu.SemaphoreType.DMA((6,)),
        ],
        compiler_params=pltpu.CompilerParams(vmem_limit_bytes=20 * 2**20),
        name="splat",
    )(*(pltpu.with_memory_space_constraint(x, pltpu.HBM) for x in (strip_map, motion, weights, frames)))
    landed = [
        pltpu.VMEM((strips >> (stage + 1), size, LANES), jnp.float32)
        for size in sizes for stage in range(bits)
    ]
    return pl.pallas_call(
        functools.partial(join_kernel, plan, group_size),
        out_shape=jax.ShapeDtypeStruct(prior_image.shape, jnp.float32),
        in_specs=[hbm] + [vmem] * (3 + len(plan)),
        out_specs=vmem,
        scratch_shapes=landed + [
            pltpu.SMEM(strip_map.shape, jnp.int32),
            pltpu.SemaphoreType.DMA(()),
            pltpu.VMEM((strips, table_rows, width), jnp.int32),
            pltpu.VMEM((3, blocks, width), jnp.int32),
            pltpu.VMEM((width, blocks), jnp.int32),
            pltpu.VMEM((width, blocks), jnp.int32),
            pltpu.VMEM((width, blocks), jnp.float32),
            pltpu.VMEM((tiles, 8, LANES), jnp.float32),
            pltpu.SemaphoreType.DMA((len(plan), bits)),
            pltpu.SemaphoreType.DMA((len(plan), bits)),
            pltpu.SemaphoreType.DMA((strips,)),
            pltpu.SemaphoreType.DMA((strips,)),
        ],
        compiler_params=pltpu.CompilerParams(
            collective_id=0, has_side_effects=True, vmem_limit_bytes=16 * 2**20
        ),
        name="join",
    )(pltpu.with_memory_space_constraint(strip_map, pltpu.HBM), table, prior_image, prior_weight, *parts)


def solution(mesh):
    in_specs = (
        P(("frame", "group"), None, None),
        P(("frame", "group"), None, None, None),
        P(("frame", "group"), None, None),
        P(),
        P(("frame", "group"), None, None),
        P(("frame", "group"), None, None),
    )
    out_specs = P(("frame", "group"), None, None)
    return jax.shard_map(
        functools.partial(body, mesh.shape["group"]), mesh=mesh, in_specs=in_specs, out_specs=out_specs,
        check_vma=False,
    )
```

```python
import functools

import jax
import jax.numpy as jnp
from jax import lax
from jax.experimental import pallas as pl
from jax.experimental.pallas import tpu as pltpu
from jax.sharding import PartitionSpec as P

MAX_SHIFT = 64
SIDE = 2
BLOCK = 32
LANES = 128
MESH = pl.DeviceIdType.MESH


def part_plan(devices, tiles):
    bits = devices.bit_length() - 1
    rest = list(range(1, bits - 1))
    count = 3
    plan = [[], []]
    for q in range(count):
        low, high = tiles * q // count, tiles * (q + 1) // count
        middle = min(high, low + ((high - low + 1) // 2 + 1) // 2 * 2)
        turn = q % len(rest)
        order = [0] + rest[turn:] + rest[:turn] + [bits - 1]
        plan[0].append((low, middle, order))
        plan[1].append((middle, high, order))
    return plan[0] + plan[1]


def splat_kernel(plan, strip_rows, map_hbm, motion_hbm, weight_hbm, frame_hbm, table_ref, *refs):
    outs = refs[: len(plan)]
    map_ref, motion_ref, weight_ref, moves_ref, scores_ref, rows_ref, up_ref, val_a, val_b, sems = refs[len(plan):]
    low_rows, low_cols = frame_hbm.shape[1:]
    grid_rows = 2 * low_rows
    bands = grid_rows // BLOCK
    strips = map_ref.shape[0]
    moved = [
        (frame_hbm.at[0], rows_ref.at[:, LANES : LANES + low_cols]),
        (motion_hbm, moves_ref), (weight_hbm, scores_ref),
        (motion_hbm, motion_ref), (weight_hbm, weight_ref), (map_hbm, map_ref),
    ]
    moved = [pltpu.make_async_copy(x, y, sems.at[n]) for n, (x, y) in enumerate(moved)]
    for copy in moved:
        copy.start()
    for acc in (val_a, val_b):
        def clear(t, carry, acc=acc):
            acc[t] = jnp.zeros(acc.shape[1:], jnp.float32)
            return carry
        lax.fori_loop(0, acc.shape[0], clear, 0)
    kk = lax.broadcasted_iota(jnp.int32, (3 * LANES, 2 * LANES), 0)
    nn = lax.broadcasted_iota(jnp.int32, (3 * LANES, 2 * LANES), 1)
    mid = (nn >> 1) + LANES
    spread = jnp.where(kk == mid, 0.75, jnp.where(kk == mid - 1 + 2 * (nn & 1), 0.25, 0.0)).astype(jnp.bfloat16)
    for copy in moved:
        copy.wait()
    block_count = moves_ref.shape[3]
    table_ref[...] = jnp.zeros(table_ref.shape, jnp.int32)
    table_ref[:bands, :block_count] = moves_ref[0, 1]
    table_ref[bands : 2 * bands, :block_count] = moves_ref[0, 0]
    table_ref[2 * bands : 3 * bands, :block_count] = scores_ref[0]
    table_ref[...] = pltpu.roll(table_ref[...], SIDE, 1)
    first = rows_ref[:, LANES : 2 * LANES].astype(jnp.float32)[:, :1]
    last = rows_ref[:, low_cols : LANES + low_cols].astype(jnp.float32)[:, LANES - 1 :]
    rows_ref[:, :LANES] = jnp.broadcast_to(first, (low_rows, LANES)).astype(jnp.bfloat16)
    rows_ref[:, LANES + low_cols :] = jnp.broadcast_to(last, (low_rows, LANES)).astype(jnp.bfloat16)
    line = lax.broadcasted_iota(jnp.int32, (low_rows, 2 * LANES), 0)
    lane = lax.broadcasted_iota(jnp.int32, (BLOCK, LANES), 1)

    def low_tile(u, carry):
        z = jnp.dot(
            rows_ref[:, pl.ds(pl.multiple_of(u * LANES, LANES), 3 * LANES)], spread,
            preferred_element_type=jnp.float32,
        )
        above = jnp.where(line == 0, z, pltpu.roll(z, 1, 0))
        below = jnp.where(line == low_rows - 1, z, pltpu.roll(z, low_rows - 1, 0))
        even = 0.75 * z + 0.25 * above
        odd = 0.75 * z + 0.25 * below
        for half in range(2):
            cols = slice(half * LANES, (half + 1) * LANES)
            up_ref[half, pl.ds(0, low_rows, stride=2), :] = even[:, cols]
            up_ref[half, pl.ds(1, low_rows, stride=2), :] = odd[:, cols]
        for half in range(2):
            for j in range(LANES // BLOCK):
                for b in range(bands):
                    column = u * (2 * LANES // BLOCK) + half * (LANES // BLOCK) + j
                    dy = motion_ref[0, 0, b, column]
                    dx = motion_ref[0, 1, b, column]
                    w = weight_ref[0, b, column].astype(jnp.float32)
                    place = LANES + column * BLOCK + dx
                    tile = place >> 7
                    start = place & (LANES - 1)
                    top = MAX_SHIFT + b * BLOCK + dy
                    block = up_ref[half, b * BLOCK : (b + 1) * BLOCK, :]
                    block = pltpu.roll(block, dx & (LANES - 1), 1) * w
                    in_a = (lane >= start) & (lane < start + BLOCK)
                    in_b = lane < start + BLOCK - LANES
                    at = pl.ds(top, BLOCK)
                    val_a[tile, at, :] += jnp.where(in_a, block, 0.0)
                    val_b[tile + 1, at, :] += jnp.where(in_b, block, 0.0)
        return carry

    lax.fori_loop(0, low_cols // LANES, low_tile, 0)

    def strip(s, carry):
        at = pl.ds(MAX_SHIFT + map_ref[s] * strip_rows, strip_rows)
        for (low, high, order), out in zip(plan, outs):
            position = 0
            for bit in order:
                position = position * 2 + ((s >> bit) & 1)
            for t in range(low, high):
                row = (t - low) * strip_rows
                out[position, row : row + strip_rows, :] = val_a[t + 1, at, :] + val_b[t + 1, at, :]
        return carry

    lax.fori_loop(0, strips, strip, 0)


def join_kernel(plan, group_size, map_hbm, table_ref, image_ref, prior_ref, *refs):
    count = len(plan)
    bits = len(plan[0][2])
    parts = refs[:count]
    out_ref = refs[count]
    landed = refs[count + 1 : count + 1 + count * bits]
    map_ref, map_sem, gathered, staged, move_x, move_y, weight, counts, send_sem, recv_sem, table_send, table_recv = refs[
        count + 1 + count * bits :
    ]
    strip_rows = out_ref.shape[1]
    tiles = out_ref.shape[2] // LANES
    devices = gathered.shape[0]
    blocks = staged.shape[1]
    bands = blocks // devices
    me = lax.axis_index("frame") * group_size + lax.axis_index("group")

    def bit_of(bit):
        return (me // 2**bit) % 2

    groups = [list(range(3, bits)), [1, 2], [0]]
    groups = [[bit for bit in group if bit < bits] for group in groups]
    peers = [[sum(2**bit for n, bit in enumerate(g) if d >> n & 1) for d in range(1, 2 ** len(g))] for g in groups]

    def partner(delta):
        other = me
        for bit in range(bits):
            if delta >> bit & 1:
                other = other + 2**bit - 2 * 2**bit * bit_of(bit)
        return (other // group_size, other % group_size)

    map_copy = pltpu.make_async_copy(map_hbm, map_ref, map_sem)
    map_copy.start()
    barrier = pltpu.get_barrier_semaphore()
    greeted = sorted(set(sum(peers, [])) | {2**bit for bit in range(bits)})
    for delta in greeted:
        pl.semaphore_signal(barrier, inc=1, device_id=partner(delta), device_id_type=MESH)
    pl.semaphore_wait(barrier, len(greeted))

    def source_of(q, stage):
        return parts[q] if stage == 0 else landed[q * bits + stage - 1]

    def copy_of(q, stage):
        source = source_of(q, stage)
        half = source.shape[0] // 2
        bit = plan[q][2][stage]
        return pltpu.make_async_remote_copy(
            src_ref=source.at[pl.ds((1 - bit_of(bit)) * half, half)],
            dst_ref=landed[q * bits + stage],
            send_sem=send_sem.at[q, stage],
            recv_sem=recv_sem.at[q, stage],
            device_id=partner(2**bit),
            device_id_type=MESH,
        )

    slot, scale, sizes = 0, 1, []
    for group in groups:
        sizes.append(scale)
        for bit in group:
            slot = slot + bit_of(bit) * scale
            scale = 2 * scale

    def table_copies_of(step):
        size = sizes[step]
        window = pl.ds(slot // size * size, size)
        return [
            pltpu.make_async_remote_copy(
                src_ref=table_ref if step == 0 else gathered.at[window],
                dst_ref=gathered.at[slot] if step == 0 else gathered.at[window],
                send_sem=table_send.at[delta],
                recv_sem=table_recv.at[delta],
                device_id=partner(delta),
                device_id_type=MESH,
            )
            for delta in peers[step]
        ]

    def turn_tables():
        for f in range(devices):
            for c in range(3):
                staged[c, f * bands : (f + 1) * bands, :] = gathered[f, c * bands : (c + 1) * bands, :]
        for low in range(0, blocks, LANES):
            high = min(blocks, low + LANES)
            for c, dest in enumerate((move_x, move_y, weight)):
                dest[:, low:high] = jnp.transpose(staged[c, low:high, :].astype(jnp.float32)).astype(dest.dtype)

    def count_tiles(first, last):
        position = map_ref[me] * strip_rows + lax.broadcasted_iota(jnp.int32, (8, blocks), 0)
        position = position - BLOCK * (lax.broadcasted_iota(jnp.int32, (8, blocks), 1) % bands)
        column = lax.broadcasted_iota(jnp.int32, (LANES, blocks), 0)
        per_tile = LANES // BLOCK

        def tile(t, carry):
            total = jnp.zeros((8, LANES), jnp.float32)
            for i in range(per_tile + 2 * SIDE):
                at = pl.ds(per_tile * t + i, 1)
                rows_in = ((position - move_y[at, :]) & -BLOCK) == 0
                cols_in = ((column - (move_x[at, :] + BLOCK * (i - SIDE))) & -BLOCK) == 0
                total = total + lax.dot_general(
                    jnp.where(rows_in, weight[at, :], 0.0).astype(jnp.bfloat16),
                    jnp.where(cols_in, 1.0, 0.0).astype(jnp.bfloat16),
                    (((1,), (1,)), ((), ())),
                    preferred_element_type=jnp.float32,
                )
            counts[t] = total
            return carry

        lax.fori_loop(first, last, tile, 0)

    copies = {}
    table_copies = [table_copies_of(step) for step in range(len(groups))]
    for copy in table_copies[0]:
        copy.start()
    for q in range(count):
        copies[q, 0] = copy_of(q, 0)
        copies[q, 0].start()
    gathered[slot] = table_ref[...]

    def next_tables(step):
        for copy in table_copies[step]:
            copy.wait_recv()
        if step + 1 < len(groups):
            for copy in table_copies[step + 1]:
                copy.start()

    count_slots = list(range(4, 2 * bits - 1))
    for stage in range(bits):
        for chunk in range(2):
            for q in range(chunk * count // 2, (chunk + 1) * count // 2):
                copies[q, stage].wait_recv()
                source = source_of(q, stage)
                half = source.shape[0] // 2
                mine = bit_of(plan[q][2][stage])
                dest = landed[q * bits + stage]
                dest[...] = dest[...] + source[pl.ds(mine * half, half)]
                if stage + 1 < bits:
                    copies[q, stage + 1] = copy_of(q, stage + 1)
                    copies[q, stage + 1].start()
            at = 2 * stage + chunk
            if at == 1:
                next_tables(0)
            if at == 3:
                next_tables(1)
            if at == 4:
                next_tables(2)
                map_copy.wait()
                turn_tables()
            if at in count_slots:
                n = count_slots.index(at)
                count_tiles(tiles * n // len(count_slots), tiles * (n + 1) // len(count_slots))
    for q, (low, high, _) in enumerate(plan):
        total = landed[q * bits + bits - 1]
        for t in range(low, high):
            row = (t - low) * strip_rows
            weighted = total[0, row : row + strip_rows, :]
            cols = slice(t * LANES, (t + 1) * LANES)
            prior = prior_ref[0, :, cols]
            out_ref[0, :, cols] = (weighted + prior * image_ref[0, :, cols]) / (counts[t, :strip_rows, :] + prior)
    for copy in list(copies.values()) + sum(table_copies, []):
        copy.wait_send()


def body(group_size, frames, motion, weights, strip_map, prior_image, prior_weight):
    low_rows, low_cols = frames.shape[1:]
    strips = strip_map.shape[0]
    strip_rows = prior_image.shape[1]
    tiles = 2 * low_cols // LANES
    plan = part_plan(strips, tiles)
    bits = len(plan[0][2])
    vmem = pl.BlockSpec(memory_space=pltpu.VMEM)
    hbm = pl.BlockSpec(memory_space=pltpu.HBM)
    sizes = [(high - low) * strip_rows for low, high, _ in plan]
    acc = pltpu.VMEM((tiles + 3, 2 * low_rows + 2 * MAX_SHIFT, LANES), jnp.float32)
    bands = motion.shape[2]
    width = -(-(motion.shape[3] + 2 * SIDE) // LANES) * LANES
    table_rows = -(-3 * bands // 8) * 8
    blocks = strips * bands
    table, *parts = pl.pallas_call(
        functools.partial(splat_kernel, plan, strip_rows),
        out_shape=[jax.ShapeDtypeStruct((table_rows, width), jnp.int32)]
        + [jax.ShapeDtypeStruct((strips, size, LANES), jnp.float32) for size in sizes],
        in_specs=[hbm] * 4,
        out_specs=[vmem] * (1 + len(plan)),
        scratch_shapes=[
            pltpu.SMEM(strip_map.shape, jnp.int32),
            pltpu.SMEM(motion.shape, jnp.int32),
            pltpu.SMEM(weights.shape, jnp.int32),
            pltpu.VMEM(motion.shape, jnp.int32),
            pltpu.VMEM(weights.shape, jnp.int32),
            pltpu.VMEM((low_rows, low_cols + 2 * LANES), jnp.bfloat16),
            pltpu.VMEM((2, 2 * low_rows, LANES), jnp.float32),
            acc, acc,
            pltpu.SemaphoreType.DMA((6,)),
        ],
        compiler_params=pltpu.CompilerParams(vmem_limit_bytes=20 * 2**20),
        name="splat",
    )(*(pltpu.with_memory_space_constraint(x, pltpu.HBM) for x in (strip_map, motion, weights, frames)))
    landed = [
        pltpu.VMEM((strips >> (stage + 1), size, LANES), jnp.float32)
        for size in sizes for stage in range(bits)
    ]
    return pl.pallas_call(
        functools.partial(join_kernel, plan, group_size),
        out_shape=jax.ShapeDtypeStruct(prior_image.shape, jnp.float32),
        in_specs=[hbm] + [vmem] * (3 + len(plan)),
        out_specs=vmem,
        scratch_shapes=landed + [
            pltpu.SMEM(strip_map.shape, jnp.int32),
            pltpu.SemaphoreType.DMA(()),
            pltpu.VMEM((strips, table_rows, width), jnp.int32),
            pltpu.VMEM((3, blocks, width), jnp.int32),
            pltpu.VMEM((width, blocks), jnp.int32),
            pltpu.VMEM((width, blocks), jnp.int32),
            pltpu.VMEM((width, blocks), jnp.float32),
            pltpu.VMEM((tiles, 8, LANES), jnp.float32),
            pltpu.SemaphoreType.DMA((len(plan), bits)),
            pltpu.SemaphoreType.DMA((len(plan), bits)),
            pltpu.SemaphoreType.DMA((strips,)),
            pltpu.SemaphoreType.DMA((strips,)),
        ],
        compiler_params=pltpu.CompilerParams(
            collective_id=0, has_side_effects=True, vmem_limit_bytes=16 * 2**20
        ),
        name="join",
    )(pltpu.with_memory_space_constraint(strip_map, pltpu.HBM), table, prior_image, prior_weight, *parts)


def solution(mesh):
    in_specs = (
        P(("frame", "group"), None, None),
        P(("frame", "group"), None, None, None),
        P(("frame", "group"), None, None),
        P(),
        P(("frame", "group"), None, None),
        P(("frame", "group"), None, None),
    )
    out_specs = P(("frame", "group"), None, None)
    return jax.shard_map(
        functools.partial(body, mesh.shape["group"]), mesh=mesh, in_specs=in_specs, out_specs=out_specs,
        check_vma=False,
    )
```
